32 devices in a mesh: dp: 4 (over x, core), expert: 8 (over z, y).
Axes of the slice: x: 2, y: 2, z: 4, core: 2. Of those that a mesh axis runs over, the one named last changes fastest.
Arguments:
- tokens: bfloat16 [6144, 1024], P(('dp', 'expert')), may hold values from -6 to 6
- norm_gain: float32 [1024], replicated, may hold values from 0.5 to 1.5
- expert_ids: int32 [6144, 2], P(('dp', 'expert')), may hold values from 0 to 7, all different within a row; in each aligned block of 192 rows (0 to 191, 192 to 383, ...) at most 72 rows name the same one
- gate_share: float32 [6144, 2], P(('dp', 'expert')), may hold values from 0.25 to 1
- w_gate: bfloat16 [8, 2048, 1024], P('expert', 'dp'), may hold values from -0.1875 to 0.1875
- w_up: bfloat16 [8, 2048, 1024], P('expert', 'dp'), may hold values from -0.1875 to 0.1875
- w_down: bfloat16 [8, 2048, 1024], P('expert', 'dp'), may hold values from -0.125 to 0.125
- out_grad: bfloat16 [6144, 1024], P(('dp', 'expert')), may hold values from -6 to 6
Outputs:
- mixed: bfloat16 [6144, 1024], P(('dp', 'expert'))
- tokens_grad: bfloat16 [6144, 1024], P(('dp', 'expert'))
- gain_grad: float32 [1024], replicated
- w_gate_grad: float32 [8, 2048, 1024], P('expert', 'dp')
- w_up_grad: float32 [8, 2048, 1024], P('expert', 'dp')
- w_down_grad: float32 [8, 2048, 1024], P('expert', 'dp')
The draws below stay inside these ranges and needn't reach their ends.
Inputs may be any that keep to these rules, and one draw needn't show every extreme that they name: `expert_ids`: each token names two different experts. In each aligned block of 192 rows (the rows of one device) no expert is named more than 72 times, a bound that some block reaches.
All inputs are finite; a program needn't handle non-finite values.
Results may differ from the reference program's by a relative error of at most 0.0095.
Values may be sent and summed in bfloat16 or wider, within the bound.
A program may use at most 128 MiB of HBM per device.

```python
import math
import jax
import jax.numpy as jnp
import numpy as np
from jax import lax

D = 1024
HIDDEN_SIZE = 2048
TOK_DEV = 192
EXPERTS = 8
REPLICAS = 4
CAP = 72
TOKENS = 6144


def steps_of(rng, dims, split, low, largest):
    factor_of = 1.0
    for dim, blocks in split:
        steps = jax.random.uniform(jax.random.fold_in(jax.random.fold_in(rng, 6), dim), (blocks,), jnp.float32, low / len(split), largest / len(split))
        factor_of = factor_of * jnp.repeat(jnp.exp(steps), dims[dim] // blocks).reshape((-1,) + (1,) * (len(dims) - 1 - dim))
    return factor_of


def deal_out(key, own, number, rows, number_of, top, limit, skew):
    sequence = jax.random.permutation(key, number_of)
    heavy_load, usual = portions_of(number_of, rows * top, limit, skew, True), portions_of(number_of, rows * top, limit, skew, False)
    places = jnp.arange(number_of)

    def named(lengths, offset_by):
        used = int((lengths > 0).sum())
        fixed = max(1, used // 4)
        passed = fixed + (places - fixed + offset_by * (used - fixed)) % max(1, number_of - fixed)
        return jnp.zeros((number_of,), jnp.int32).at[sequence[jnp.where(places < fixed, places, passed)]].set(jnp.asarray(lengths, jnp.int32))

    lengths = jnp.where(number % 4 == 0, named(heavy_load, number // 4), named(usual, number - number // 4 - 1))
    mixed = jax.random.permutation(jax.random.fold_in(own, 3), number_of)
    source_of, receiver = mixed[0:number_of // 2 * 2:2], mixed[1:number_of // 2 * 2:2]
    slack = jnp.minimum(lengths[source_of] - 1, limit - lengths[receiver]) // 2
    slack = jnp.where((source_of == sequence[0]) | (receiver == sequence[0]) | (lengths[receiver] == 0), 0, jnp.maximum(slack, 0))
    passed = jax.random.randint(jax.random.fold_in(own, 4), (number_of // 2,), 0, 1 << 20) % (slack + 1)
    lengths = lengths.at[source_of].add(-passed).at[receiver].add(passed)
    items = jnp.searchsorted(jnp.cumsum(lengths), jnp.arange(rows * top), side="right").astype(jnp.int32)
    grid = items.reshape(top, rows).T
    grid = grid[jax.random.permutation(jax.random.fold_in(own, 1), rows)]
    offset_by = jax.random.randint(jax.random.fold_in(own, 2), (rows, 1), 0, top)
    return jnp.take_along_axis(grid, (jnp.arange(top)[None, :] + offset_by) % top, axis=1)


def portions_of(amount, total, bound, skew, full):
    weights = [(1 << 20) // math.isqrt(rank ** skew) + 1 for rank in range(1, amount + 1)]
    largest = bound if full else min(bound, max(-(-total // amount), total * weights[0] // sum(weights)))
    least = 1 if total - largest >= amount - 1 else 0
    given, spare = [largest] + [least] * (amount - 1), total - largest - least * (amount - 1)
    while spare > 0:
        free = [i for i in range(1, amount) if given[i] < largest] or [i for i in range(1, amount) if given[i] < bound]
        pool, budget = sum([weights[i] for i in free]), spare
        for i in free:
            more = min(bound - given[i], max(1, budget * weights[i] // pool), spare)
            given[i] = given[i] + more
            spare = spare - more
    return np.array(given)


def normal_values(own_key, extent, deviation, bound, shards=(), kind=jnp.bfloat16):
    level = steps_of(own_key, extent, shards, -0.22, 0.18) if shards else 1.0
    entries = jax.random.normal(own_key, extent, jnp.float32) * deviation * level
    return jnp.minimum(jnp.maximum(entries, -bound), bound).astype(kind)


def setup_inputs(seed: int = 0) -> dict:
    splits = jax.random.split(jax.random.key(seed), 9)
    tokens = normal_values(splits[0], (TOKENS, D), 1.0, 6.0, ((0, 32),))
    norm_gain = jnp.clip(1.0 + 0.1 * jax.random.normal(splits[1], (D,), jnp.float32), 0.5, 1.5)
    expert_ids_keys = jax.random.split(jax.random.fold_in(splits[2], 1), TOKENS // TOK_DEV)
    expert_ids_turns = jax.random.permutation(jax.random.fold_in(splits[2], 3), TOKENS // TOK_DEV)
    expert_ids = jax.vmap(lambda own, number: deal_out(jax.random.fold_in(splits[2], 2), own, number, TOK_DEV, EXPERTS, 2, CAP, 2))(expert_ids_keys, expert_ids_turns).reshape((TOKENS, 2))
    gate_share = jnp.clip(0.25 + 0.75 * jax.random.uniform(splits[3], (TOKENS, 2), jnp.float32) ** steps_of(splits[3], (TOKENS, 2), ((0, 32),), -0.2, 0.2), 0.25, 1.0)
    w_gate = normal_values(splits[4], (EXPERTS, HIDDEN_SIZE, D), D ** -0.5, 0.1875, ((0, 8), (1, 4)))
    w_up = normal_values(splits[5], (EXPERTS, HIDDEN_SIZE, D), D ** -0.5, 0.1875, ((0, 8), (1, 4)))
    w_down = normal_values(splits[6], (EXPERTS, HIDDEN_SIZE, D), HIDDEN_SIZE ** -0.5, 0.125, ((0, 8), (1, 4)))
    out_grad = normal_values(splits[7], (TOKENS, D), 1.0, 6.0, ((0, 32),))
    return {"tokens": tokens, "norm_gain": norm_gain, "expert_ids": expert_ids, "gate_share": gate_share, "w_gate": w_gate, "w_up": w_up, "w_down": w_down, "out_grad": out_grad}


epsilon = 1e-05
contract_last = (((1,), (1,)), ((), ()))
contract_first = (((0,), (0,)), ((), ()))

def pair_slots(expert_block, experts_n, capacity):
    flat_ids = expert_block.reshape(-1).astype(jnp.int32)
    onehot = (flat_ids[:, None] == jnp.arange(experts_n, dtype=jnp.int32)[None, :]).astype(jnp.int32)
    earlier = jnp.cumsum(onehot, axis=0) - onehot
    rank_ids = lax.optimization_barrier(jnp.sum(earlier * onehot, axis=1))
    return (flat_ids * capacity + rank_ids).astype(jnp.int32)

def expert_inner(in_rows, cot_rows, gate_weight, up_weight, down_weight):
    gate_pre = lax.dot_general(in_rows, gate_weight, contract_last, preferred_element_type=jnp.float32)
    up_pre = lax.dot_general(in_rows, up_weight, contract_last, preferred_element_type=jnp.float32)
    sigmoid_gate = jax.nn.sigmoid(gate_pre)
    activated = gate_pre * sigmoid_gate
    hidden = (activated * up_pre).astype(jnp.bfloat16)
    hidden_grad = lax.dot_general(cot_rows, down_weight, contract_last, preferred_element_type=jnp.float32)
    up_grad = (hidden_grad * activated).astype(jnp.bfloat16)
    gate_grad = (hidden_grad * up_pre * sigmoid_gate * (1.0 + gate_pre * (1.0 - sigmoid_gate))).astype(jnp.bfloat16)
    return (hidden, gate_grad, up_grad)

def expert_outer(hidden, gate_grad, up_grad, gate_weight, up_weight, down_weight):
    out_part = jnp.dot(hidden, down_weight, preferred_element_type=jnp.float32)
    input_part = jnp.dot(gate_grad, gate_weight, preferred_element_type=jnp.float32) + jnp.dot(up_grad, up_weight, preferred_element_type=jnp.float32)
    return (out_part, input_part)

def contract_rows(left, right):
    return lax.dot_general(left, right, contract_first, preferred_element_type=jnp.float32)

def reference(tokens, norm_gain, expert_ids, gate_share, w_gate, w_up, w_down, out_grad):
    blocks_n = REPLICAS * EXPERTS
    slot_count = EXPERTS * CAP
    tok_float = tokens.astype(jnp.float32)
    inv_rms = lax.rsqrt(lax.optimization_barrier(jnp.mean(tok_float * tok_float, axis=1, keepdims=True)) + epsilon)
    normed = (tok_float * inv_rms * norm_gain[None, :]).astype(jnp.bfloat16)
    pair_cot = (gate_share[:, :, None] * out_grad.astype(jnp.float32)[:, None, :]).astype(jnp.bfloat16).reshape(2 * TOKENS, D)
    slot_ids = jax.vmap(lambda block: pair_slots(block, EXPERTS, CAP))(expert_ids.reshape(blocks_n, TOK_DEV, 2))
    block_index = jnp.arange(blocks_n, dtype=jnp.int32)[:, None] * jnp.ones((1, 2 * TOK_DEV), jnp.int32)
    pair_index = jnp.arange(2 * TOKENS, dtype=jnp.int32).reshape(blocks_n, 2 * TOK_DEV)
    slot_table = jnp.full((blocks_n, slot_count), 2 * TOKENS, jnp.int32).at[block_index, slot_ids].set(pair_index)
    slot_table = slot_table.reshape(REPLICAS, EXPERTS, EXPERTS, CAP).transpose(2, 0, 1, 3).reshape(EXPERTS, REPLICAS * slot_count)
    normed_pad = jnp.concatenate([normed, jnp.zeros((1, D), jnp.bfloat16)], axis=0)
    cot_pad = jnp.concatenate([pair_cot, jnp.zeros((1, D), jnp.bfloat16)], axis=0)

    def one_expert(operands):
        table_row, gate_weight, up_weight, down_weight = operands
        in_rows = normed_pad[table_row // 2]
        cot_rows = cot_pad[table_row]
        hidden, gate_grad, up_grad = expert_inner(in_rows, cot_rows, gate_weight, up_weight, down_weight)
        out_part, input_part = expert_outer(hidden, gate_grad, up_grad, gate_weight, up_weight, down_weight)
        return (out_part.astype(jnp.bfloat16), input_part.astype(jnp.bfloat16), contract_rows(gate_grad, in_rows), contract_rows(up_grad, in_rows), contract_rows(hidden, cot_rows))
    expert_out, expert_dx, w_gate_grad, w_up_grad, w_down_grad = lax.map(one_expert, (slot_table, w_gate, w_up, w_down))
    expert_index = slot_ids // CAP
    place_index = (expert_index * (REPLICAS * slot_count) + block_index * CAP + slot_ids % CAP).reshape(-1).astype(jnp.int32)
    out_pairs = expert_out.reshape(-1, D)[place_index].astype(jnp.float32).reshape(TOKENS, 2, D)
    dx_pairs = expert_dx.reshape(-1, D)[place_index].astype(jnp.float32).reshape(TOKENS, 2, D)
    mixture = lax.optimization_barrier(jnp.sum(gate_share[:, :, None] * out_pairs, axis=1))
    mixed = (tok_float + mixture).astype(jnp.bfloat16)
    normed_grad = lax.optimization_barrier(jnp.sum(dx_pairs, axis=1))
    gain_grad = lax.optimization_barrier(jnp.sum(normed_grad * tok_float * inv_rms, axis=0))
    scaled = normed_grad * norm_gain[None, :]
    inner_mean = lax.optimization_barrier(jnp.mean(scaled * tok_float, axis=1, keepdims=True))
    tokens_grad = (out_grad.astype(jnp.float32) + inv_rms * scaled - inv_rms * inv_rms * inv_rms * tok_float * inner_mean).astype(jnp.bfloat16)
    return (mixed, tokens_grad, gain_grad, w_gate_grad, w_up_grad, w_down_grad)
```

```python
import jax
import jax.numpy as jnp
from jax import lax
from jax.sharding import PartitionSpec as P

epsilon = 1e-05
contract_last = (((1,), (1,)), ((), ()))
contract_first = (((0,), (0,)), ((), ()))


def pair_slots(expert_block, experts_n, capacity):
    flat_ids = expert_block.reshape(-1)
    onehot = (flat_ids[:, None] == jnp.arange(experts_n, dtype=jnp.int32)[None, :]).astype(
        jnp.int32
    )
    earlier = jnp.cumsum(onehot, axis=0) - onehot
    rank_ids = jnp.sum(earlier * onehot, axis=1)
    return flat_ids * capacity + rank_ids


def expert_inner(in_rows, cot_rows, gate_weight, up_weight, down_weight):
    gate_pre = lax.dot_general(
        in_rows, gate_weight, contract_last, preferred_element_type=jnp.float32
    )
    up_pre = lax.dot_general(in_rows, up_weight, contract_last, preferred_element_type=jnp.float32)
    sigmoid_gate = jax.nn.sigmoid(gate_pre)
    activated = gate_pre * sigmoid_gate
    hidden = (activated * up_pre).astype(jnp.bfloat16)
    hidden_grad = lax.dot_general(
        cot_rows, down_weight, contract_last, preferred_element_type=jnp.float32
    )
    up_grad = (hidden_grad * activated).astype(jnp.bfloat16)
    gate_grad = (
        hidden_grad * up_pre * sigmoid_gate * (1.0 + gate_pre * (1.0 - sigmoid_gate))
    ).astype(jnp.bfloat16)
    return (hidden, gate_grad, up_grad)


def expert_outer(hidden, gate_grad, up_grad, gate_weight, up_weight, down_weight):
    out_part = jnp.dot(hidden, down_weight, preferred_element_type=jnp.float32)
    input_part = jnp.dot(gate_grad, gate_weight, preferred_element_type=jnp.float32) + jnp.dot(
        up_grad, up_weight, preferred_element_type=jnp.float32
    )
    return (out_part, input_part)


def contract_rows(left, right):
    return lax.dot_general(left, right, contract_first, preferred_element_type=jnp.float32)


def sum_all(value, axes):
    total = value.reshape(8, -1)
    for axis in axes:
        size, step = lax.axis_size(axis), 1
        assert size & (size - 1) == 0
        while step < size:
            total = total + lax.ppermute(total, axis, [(i, i ^ step) for i in range(size)])
            step *= 2
    return total.reshape(value.shape)


def layer_step(tokens, norm_gain, expert_ids, gate_share, w_gate, w_up, w_down, out_grad):
    tok_rows, feature_width = tokens.shape
    experts_n = lax.axis_size("expert")
    capacity = 3 * tok_rows // experts_n
    slot_count = experts_n * capacity
    tok_float = tokens.astype(jnp.float32)
    inv_rms = lax.rsqrt(jnp.mean(tok_float * tok_float, axis=1, keepdims=True) + epsilon)
    normed = (tok_float * inv_rms * norm_gain[None, :]).astype(jnp.bfloat16)
    pair_cot = (
        (gate_share[:, :, None] * out_grad.astype(jnp.float32)[:, None, :])
        .astype(jnp.bfloat16)
        .reshape(2 * tok_rows, feature_width)
    )
    slot_ids = pair_slots(expert_ids, experts_n, capacity)
    matches = jnp.arange(slot_count, dtype=jnp.int32)[:, None] == slot_ids[None, :]
    pair_place = matches.astype(jnp.bfloat16)
    token_place = jnp.any(matches.reshape(slot_count, tok_rows, 2), axis=2).astype(jnp.bfloat16)
    send_rows = jnp.dot(token_place, normed, preferred_element_type=jnp.float32).astype(
        jnp.bfloat16
    )
    send_cot = jnp.dot(pair_place, pair_cot, preferred_element_type=jnp.float32).astype(
        jnp.bfloat16
    )
    in_rows = lax.all_to_all(send_rows, "expert", split_axis=0, concat_axis=0, tiled=True)
    cot_rows = lax.all_to_all(send_cot, "expert", split_axis=0, concat_axis=0, tiled=True)
    gate_own, up_own, down_own = (w_gate[0], w_up[0], w_down[0])
    across = [(i, i ^ 2) for i in range(lax.axis_size("dp"))]
    beside = [(i, i ^ 1) for i in range(lax.axis_size("dp"))]

    def far(value):
        return lax.ppermute(value, "dp", across)

    def near(value):
        return lax.ppermute(value, "dp", beside)

    gate_far = far(gate_own)
    up_far = far(up_own)
    down_far = far(down_own)
    local = [jnp.concatenate([own, near(own)], axis=0) for own in (gate_own, up_own, down_own)]
    diagonals = [near(value) for value in (gate_far, up_far, down_far)]
    remote = [
        jnp.concatenate(pair, axis=0) for pair in zip((gate_far, up_far, down_far), diagonals)
    ]
    own_units = gate_own.shape[0]
    remote_block = expert_inner(in_rows, cot_rows, *remote)
    local_block = expert_inner(in_rows, cot_rows, *local)

    def partials(block):
        hidden, gate_grad, up_grad = block
        return [
            contract_rows(left, right).astype(jnp.bfloat16)
            for left, right in ((hidden, cot_rows), (gate_grad, in_rows), (up_grad, in_rows))
        ]

    summed = []
    for product in partials(remote_block):
        other = near(product[own_units:]).astype(jnp.float32)
        summed.append((product[:own_units].astype(jnp.float32) + other).astype(jnp.bfloat16))
    arrived = [far(summed[0])]
    arrived.append(far(summed[1]))
    arrived.append(far(summed[2]))
    local_products = partials(local_block)
    w_down_grad, w_gate_grad, w_up_grad = (
        (
            product[:own_units].astype(jnp.float32)
            + near(product[own_units:]).astype(jnp.float32)
            + landed.astype(jnp.float32)
        )[None]
        for product, landed in zip(local_products, arrived)
    )
    remote_out, remote_input = expert_outer(*remote_block, *remote)
    local_out, local_input = expert_outer(*local_block, *local)
    out_rows = (remote_out + local_out).astype(jnp.bfloat16)
    input_rows = (remote_input + local_input).astype(jnp.bfloat16)
    back_input = lax.all_to_all(input_rows, "expert", split_axis=0, concat_axis=0, tiled=True)
    back_out = lax.all_to_all(out_rows, "expert", split_axis=0, concat_axis=0, tiled=True)
    out_pairs = contract_rows(pair_place, back_out).reshape(tok_rows, 2, feature_width)
    input_pairs = contract_rows(pair_place, back_input).reshape(tok_rows, 2, feature_width)
    mixture = jnp.sum(gate_share[:, :, None] * out_pairs, axis=1)
    mixed = (tok_float + mixture).astype(jnp.bfloat16)
    normed_grad = jnp.sum(input_pairs, axis=1)
    gain_grad = sum_all(jnp.sum(normed_grad * tok_float * inv_rms, axis=0), ("expert", "dp"))
    scaled = normed_grad * norm_gain[None, :]
    inner_mean = jnp.mean(scaled * tok_float, axis=1, keepdims=True)
    tokens_grad = (
        out_grad.astype(jnp.float32)
        + inv_rms * scaled
        - inv_rms * inv_rms * inv_rms * tok_float * inner_mean
    ).astype(jnp.bfloat16)
    return (mixed, tokens_grad, gain_grad, w_gate_grad, w_up_grad, w_down_grad)


def solution(mesh):
    in_specs = (
        P(("dp", "expert"), None),
        P(),
        P(("dp", "expert"), None),
        P(("dp", "expert"), None),
        P("expert", "dp", None),
        P("expert", "dp", None),
        P("expert", "dp", None),
        P(("dp", "expert"), None),
    )
    out_specs = (
        P(("dp", "expert"), None),
        P(("dp", "expert"), None),
        P(),
        P("expert", "dp", None),
        P("expert", "dp", None),
        P("expert", "dp", None),
    )
    return jax.shard_map(
        layer_step, mesh=mesh, in_specs=in_specs, out_specs=out_specs, check_vma=False
    )
```
